512 devices in a mesh: rep: 4 (over x), node: 16 (over y, core), local: 8 (over z).
Axes of the slice: x: 4, y: 8, z: 8, core: 2. Of those that a mesh axis runs over, the one named last changes fastest.
Arguments:
- tokens: bfloat16 [8192, 4096], P(('rep', 'node', 'local')), may hold values from -6 to 6
- expert_ids: int32 [8192, 8], P(('rep', 'node', 'local')), may hold values from 0 to 127, all different within a row; in each aligned block of 16 rows (0 to 15, 16 to 31, ...) at most 2 rows name the same one
- route_weights: float32 [8192, 8], P(('rep', 'node', 'local')), may hold values from 0.1 to 1
- gate_weight: bfloat16 [128, 768, 4096], P(('node', 'local'), 'rep'), may hold values from -0.09375 to 0.09375
- up_weight: bfloat16 [128, 768, 4096], P(('node', 'local'), 'rep'), may hold values from -0.09375 to 0.09375
- down_weight: bfloat16 [128, 768, 4096], P(('node', 'local'), None, 'rep'), may hold values from -0.21875 to 0.21875
Outputs:
- mixed_rows: bfloat16 [8192, 4096], P(('rep', 'node', 'local'))
The draws below stay inside these ranges and needn't reach their ends.
Inputs may be any that keep to these rules, and one draw needn't show every extreme that they name: `expert_ids`: each row names 8 different experts. Among the rows of one device (aligned blocks of 16 rows) no expert is named by more than 2 rows, and in some blocks some expert is named by exactly 2 rows.
All inputs are finite; a program needn't handle non-finite values.
Results may differ from the reference program's by a relative error of at most 0.0057.
Values may be sent and summed in bfloat16 or wider, within the bound.
A program may use at most 64 MiB of HBM per device.

```python
import math
import jax
import jax.numpy as jnp
import numpy as np
from jax import lax

D = 4096
FF = 768
TOP = 8
ROWS_DEV = 16
EXPERTS = 128
CAP = 2
ROWS = 8192
N_REP = 4


def block_scale(key, dims, pieces, low, largest):
    gain = 1.0
    for position, shards_of in pieces:
        steps = jax.random.uniform(jax.random.fold_in(jax.random.fold_in(key, 6), position), (shards_of,), jnp.float32, low / len(pieces), largest / len(pieces))
        gain = gain * jnp.repeat(jnp.exp(steps), dims[position] // shards_of).reshape((-1,) + (1,) * (len(dims) - 1 - position))
    return gain


def deal_out(stream_key, own, number, rows, amount, top, bound, skew):
    ranking = jax.random.permutation(stream_key, amount)
    packed, common = portions_of(amount, rows * top, bound, skew, True), portions_of(amount, rows * top, bound, skew, False)
    places = jnp.arange(amount)

    def named(sizes, offset_by):
        used = int((sizes > 0).sum())
        fixed = max(1, used // 4)
        moved = fixed + (places - fixed + offset_by * (used - fixed)) % max(1, amount - fixed)
        return jnp.zeros((amount,), jnp.int32).at[ranking[jnp.where(places < fixed, places, moved)]].set(jnp.asarray(sizes, jnp.int32))

    sizes = jnp.where(number % 4 == 0, named(packed, number // 4), named(common, number - number // 4 - 1))
    mixed = jax.random.permutation(jax.random.fold_in(own, 3), amount)
    donor, sink = mixed[0:amount // 2 * 2:2], mixed[1:amount // 2 * 2:2]
    margin = jnp.minimum(sizes[donor] - 1, bound - sizes[sink]) // 2
    margin = jnp.where((donor == ranking[0]) | (sink == ranking[0]) | (sizes[sink] == 0), 0, jnp.maximum(margin, 0))
    moved = jax.random.randint(jax.random.fold_in(own, 4), (amount // 2,), 0, 1 << 20) % (margin + 1)
    sizes = sizes.at[donor].add(-moved).at[sink].add(moved)
    labels = jnp.searchsorted(jnp.cumsum(sizes), jnp.arange(rows * top), side="right").astype(jnp.int32)
    table = labels.reshape(top, rows).T
    table = table[jax.random.permutation(jax.random.fold_in(own, 1), rows)]
    offset_by = jax.random.randint(jax.random.fold_in(own, 2), (rows, 1), 0, top)
    return jnp.take_along_axis(table, (jnp.arange(top)[None, :] + offset_by) % top, axis=1)


def portions_of(count, total, most, skew, full):
    loads = [(1 << 20) // math.isqrt(rank ** skew) + 1 for rank in range(1, count + 1)]
    largest = most if full else min(most, max(-(-total // count), total * loads[0] // sum(loads)))
    least = 1 if total - largest >= count - 1 else 0
    counts, spare = [largest] + [least] * (count - 1), total - largest - least * (count - 1)
    while spare > 0:
        movable = [i for i in range(1, count) if counts[i] < largest] or [i for i in range(1, count) if counts[i] < most]
        pool, remaining = sum([loads[i] for i in movable]), spare
        for i in movable:
            extra = min(most - counts[i], max(1, remaining * loads[i] // pool), spare)
            counts[i] = counts[i] + extra
            spare = spare - extra
    return np.array(counts)


def noise(key, shape, spread, limit, shards=(), kind=jnp.bfloat16):
    entries = jax.random.normal(key, shape, jnp.float32) * spread
    if len(shards) > 0:
        entries = block_scale(key, shape, shards, -0.22, 0.18) * entries
    return jnp.clip(entries, min=-limit, max=limit).astype(kind)


def setup_inputs(seed: int = 0) -> dict:
    arg_keys = jax.random.split(jax.random.key(seed), 7)
    tokens = noise(arg_keys[0], (ROWS, D), 1.0, 6.0, ((0, 512),))
    expert_ids_keys = jax.random.split(jax.random.fold_in(arg_keys[1], 1), ROWS // ROWS_DEV)
    expert_ids_turns = jax.random.permutation(jax.random.fold_in(arg_keys[1], 3), ROWS // ROWS_DEV)
    expert_ids = jax.vmap(lambda own, number: deal_out(jax.random.fold_in(arg_keys[1], 2), own, number, ROWS_DEV, EXPERTS, TOP, CAP, 2))(expert_ids_keys, expert_ids_turns).reshape((ROWS, TOP))
    route_weights = jnp.clip(jnp.exp(math.log(1.0) - 2.3025851 * jax.random.uniform(arg_keys[2], (ROWS, TOP), jnp.float32) ** block_scale(arg_keys[2], (ROWS, TOP), ((0, 512),), -0.2, 0.2)), 0.1, 1.0)
    gate_weight = noise(arg_keys[3], (EXPERTS, FF, D), D ** -0.5, 0.09375, ((0, 128), (1, 4)))
    up_weight = noise(arg_keys[4], (EXPERTS, FF, D), D ** -0.5, 0.09375, ((0, 128), (1, 4)))
    down_weight = noise(arg_keys[5], (EXPERTS, FF, D), FF ** -0.5, 0.21875, ((0, 128), (2, 4)))
    return dict(tokens=tokens, expert_ids=expert_ids, route_weights=route_weights, gate_weight=gate_weight, up_weight=up_weight, down_weight=down_weight)


def reference(tokens, expert_ids, route_weights, gate_weight, up_weight, down_weight):
    row_total = tokens.shape[0]
    most_rows = N_REP * EXPERTS * CAP
    feature_dims = (((1,), (1,)), ((), ()))

    def one_expert(expert, output):
        named = expert_ids == expert
        hit_rows = jnp.any(named, axis=1)
        picked = jnp.nonzero(hit_rows, size=most_rows, fill_value=0)[0].astype(jnp.int32)
        valid = jnp.arange(most_rows) < jnp.sum(hit_rows.astype(jnp.int32))
        share = jnp.sum(jnp.where(named, route_weights, jnp.zeros_like(route_weights)), axis=1)[picked]
        chosen = tokens[picked]
        gate_vals = lax.dot_general(chosen, gate_weight[expert], feature_dims, preferred_element_type=jnp.float32)
        up_vals = lax.dot_general(chosen, up_weight[expert], feature_dims, preferred_element_type=jnp.float32)
        hidden = (jax.nn.silu(gate_vals) * up_vals).astype(jnp.bfloat16)
        result = jnp.dot(hidden, down_weight[expert], preferred_element_type=jnp.float32).astype(jnp.bfloat16)
        term = share[:, None] * result.astype(jnp.float32)
        term = jnp.where(valid[:, None], term, jnp.zeros_like(term))
        return output.at[picked].add(term)

    output = lax.fori_loop(0, EXPERTS, one_expert, jnp.zeros((row_total, D), jnp.float32))
    return output.astype(jnp.bfloat16)
```

```python
import jax
import jax.numpy as jnp
from jax import lax
from jax.sharding import PartitionSpec as P


def slot_table(expert_ids, expert_count, slot_cap):
    row_count, top_count = expert_ids.shape
    flat_ids = expert_ids.reshape(-1)
    same = flat_ids[:, None] == flat_ids[None, :]
    place = jnp.arange(row_count * top_count, dtype=jnp.int32)
    rank_of = jnp.sum((same & (place[None, :] < place[:, None])).astype(jnp.int32), axis=1)
    return (flat_ids * slot_cap + rank_of).reshape(row_count, top_count)


def route_slots(blocks):
    return lax.all_to_all(blocks, ("node", "local"), split_axis=1, concat_axis=1, tiled=True)


def on_device(tokens, expert_ids, route_weights, gate_weight, up_weight, down_weight):
    row_count, top_count = expert_ids.shape
    model_width = tokens.shape[1]
    node_count = lax.axis_size("node")
    plane_count = lax.axis_size("rep")
    expert_count = node_count * lax.axis_size("local")
    slot_cap = min(row_count, max(2, 2 * row_count * top_count // expert_count))
    slot_total = expert_count * slot_cap
    slot_of = slot_table(expert_ids, expert_count, slot_cap)
    slot_iota = jnp.arange(slot_total, dtype=jnp.int32)
    placed = jnp.any(slot_of[None, :, :] == slot_iota[:, None, None], axis=2).astype(jnp.bfloat16)
    outgoing = jnp.dot(placed, tokens, preferred_element_type=jnp.float32).astype(jnp.bfloat16)
    mixing = jnp.sum(
        jnp.where(slot_of[:, :, None] == slot_iota[None, None, :], route_weights[:, :, None], 0.0),
        axis=1,
    )
    arrived = route_slots(outgoing.reshape(1, expert_count, slot_cap, model_width))
    arrived = arrived.reshape(slot_total, model_width)
    gate_local = gate_weight[0]
    up_local = up_weight[0]
    down_local = down_weight[0]
    quarter_width = down_local.shape[1]
    feature_dims = (((1,), (1,)), ((), ()))
    shard_piece = lax.all_gather(arrived, "rep", axis=0, tiled=True)
    gate_part = lax.dot_general(
        shard_piece, gate_local, feature_dims, preferred_element_type=jnp.float32
    )
    up_part = lax.dot_general(
        shard_piece, up_local, feature_dims, preferred_element_type=jnp.float32
    )
    hidden_part = (jax.nn.silu(gate_part) * up_part).astype(jnp.bfloat16)
    expert_out = jnp.dot(
        lax.all_gather(hidden_part, "rep", axis=1, tiled=True),
        down_local,
        preferred_element_type=jnp.float32,
    ).astype(jnp.bfloat16)
    own_slots = lax.all_to_all(
        expert_out.reshape(plane_count, slot_total, quarter_width),
        "rep",
        split_axis=0,
        concat_axis=2,
        tiled=True,
    )
    returned = route_slots(own_slots.reshape(1, expert_count, slot_cap, model_width))
    back_rows = returned.reshape(slot_total, model_width).astype(jnp.float32)
    mixed_rows = jnp.dot(mixing, back_rows, precision=lax.Precision.HIGHEST)
    return mixed_rows.astype(jnp.bfloat16)


def solution(mesh):
    placed = (
        P(("rep", "node", "local"), None),
        P(("rep", "node", "local"), None),
        P(("rep", "node", "local"), None),
        P(("node", "local"), "rep", None),
        P(("node", "local"), "rep", None),
        P(("node", "local"), None, "rep"),
    )
    return jax.shard_map(
        on_device,
        mesh=mesh,
        in_specs=placed,
        out_specs=P(("rep", "node", "local"), None),
        check_vma=False,
    )
```

```python
import functools

import jax
import jax.numpy as jnp
from jax import lax
from jax.experimental import pallas as pl
from jax.experimental.pallas import tpu as pltpu
from jax.sharding import PartitionSpec as P

MESH = pl.DeviceIdType.MESH
BF, F32 = jnp.bfloat16, jnp.float32
META = 128


def near_first(ring):
    order = [0]
    for step in range(1, ring // 2 + 1):
        order += [step] if 2 * step == ring else [step, ring - step]
    return order


def kernel(dims, tok_ref, meta_ref, gate_ref, up_ref, down_ref, out_ref, *scratch):
    planes, ring, block, top, width, hidden = dims
    (
        rows_all, outgoing, arrived, weights, down, psend, pown, precv, hid, outs,
        returned, mix_hi, mix_lo, zsend, zrecv, fin, cols,
        s_x, r_x, s_m, r_m, s_w, r_w, s_ag, r_ag, s_a, r_a, s_p, r_p, s_h, r_h,
        s_b, r_b, s_z, r_z, s_f, r_f, l_sem,
    ) = scratch
    quarter = hidden // planes
    rows = planes * block
    slots = planes * 2
    msgs = 2 * ring
    msg_rows = ring * slots
    order = near_first(ring)
    back = [order.index((ring - d) % ring) for d in order]

    r = lax.axis_index("rep")
    node = lax.axis_index("node")
    z = lax.axis_index("local")
    y, c = node // 2, node % 2

    def x_peer(step):
        return ((r + step) % planes, node, z)

    def along(step, role, core):
        yy = (y + step * (1 - role)) % ring
        zz = (z + step * role) % ring
        return (r, 2 * yy + core, zz)

    def remote(src, dst, send, recv, device):
        return pltpu.make_async_remote_copy(
            src_ref=src, dst_ref=dst, send_sem=send, recv_sem=recv,
            device_id=device, device_id_type=MESH,
        )

    barrier = pltpu.get_barrier_semaphore()
    partners = [x_peer(s) for s in range(1, planes)]
    partners += [(r, 2 * y + (c + 1) % 2, z)]
    for d in range(1, ring):
        for core in range(2):
            partners += [along(d, 0, core), along(d, 1, core)]
    for p in partners:
        pl.semaphore_signal(barrier, inc=1, device_id=p, device_id_type=MESH)
    pl.semaphore_wait(barrier, len(partners))

    def col(p):
        return pl.ds(pl.multiple_of(p * width, 128), width)

    def row16(p, n=block):
        return pl.ds(pl.multiple_of(p * n, 16), n)

    def x_copies(step):
        p = (r + step) % planes
        here = row16(r)
        return (
            remote(tok_ref.at[:, col(p)], rows_all.at[0, here, pl.ds(0, width)],
                   s_x.at[step], r_x.at[step], x_peer(step)),
            remote(meta_ref, rows_all.at[0, here, pl.ds(width, META)],
                   s_m.at[step], r_m.at[step], x_peer(step)),
        )

    for step in range(1, planes):
        for cp in x_copies(step):
            cp.start()
    own_tok = pltpu.make_async_copy(tok_ref.at[:, col(r)], rows_all.at[0, row16(r), pl.ds(0, width)], l_sem.at[0])
    own_meta = pltpu.make_async_copy(meta_ref, rows_all.at[0, row16(r), pl.ds(width, META)], l_sem.at[1])
    own_tok.start()
    own_meta.start()

    def w_copies(step):
        p = (r + step) % planes
        here = row16(r, quarter)
        return (
            remote(gate_ref.at[0, :, col(p)], weights.at[0, here, :], s_w.at[0, step], r_w.at[0, step], x_peer(step)),
            remote(up_ref.at[0, :, col(p)], weights.at[1, here, :], s_w.at[1, step], r_w.at[1, step], x_peer(step)),
        )

    for step in range(1, planes):
        for cp in w_copies(step):
            cp.start()
    own_gate = pltpu.make_async_copy(gate_ref.at[0, :, col(r)], weights.at[0, row16(r, quarter), :], l_sem.at[2])
    own_up = pltpu.make_async_copy(up_ref.at[0, :, col(r)], weights.at[1, row16(r, quarter), :], l_sem.at[3])
    own_down = pltpu.make_async_copy(down_ref.at[0], down, l_sem.at[4])
    own_gate.start()
    own_up.start()
    own_down.start()

    own_tok.wait()
    own_meta.wait()
    for step in range(1, planes):
        for cp in x_copies(step):
            cp.wait_recv()

    def ag_copy(d):
        return remote(rows_all.at[0], rows_all.at[d and ring - d], s_ag.at[d], r_ag.at[d], along(d, 1 - c, c))

    for d in order[1:]:
        ag_copy(d).start()

    lanes = msgs * 2 * slots
    shape = (2 * rows, lanes)
    t = lax.broadcasted_iota(jnp.int32, shape, 0)
    q = lax.broadcasted_iota(jnp.int32, shape, 1)
    j = q // (2 * slots)
    pos, dc = j // 2, j % 2
    d_of = jnp.where(pos % 2 == 1, (pos + 1) // 2, (ring - pos // 2) % ring)
    expert = (2 * ((y + d_of * (1 - c)) % ring) + (c + dc) % 2) * ring + (z + d_of * c) % ring
    expert = expert.astype(F32)
    same_block = (t // rows) == ((q // slots) % 2)
    slot_left = ((q % slots) - 2 * ((t // block) % planes)).astype(F32)
    a = lax.broadcasted_iota(jnp.int32, (2 * rows, 2 * rows), 0)
    b = lax.broadcasted_iota(jnp.int32, (2 * rows, 2 * rows), 1)
    earlier = jnp.where((b < a) & (a // block == b // block), 1.0, 0.0).astype(BF)

    for pair in range(ring // 2):
        for d in (2 * pair, 2 * pair + 1):
            if d:
                ag_copy((ring - d) % ring).wait_recv()
        both = rows_all[2 * pair:2 * pair + 2].reshape(2 * rows, width + META)
        meta = both[:, width:].astype(F32)
        hits = jnp.zeros(shape, F32)
        high = jnp.zeros(shape, F32)
        low = jnp.zeros(shape, F32)
        for k in range(top):
            named = (meta[:, k:k + 1] == expert) & same_block
            hits = jnp.where(named, 1.0, hits)
            high = jnp.where(named, meta[:, top + k:top + k + 1], high)
            low = jnp.where(named, meta[:, 2 * top + k:2 * top + k + 1], low)
        rank = jnp.dot(earlier, hits.astype(BF), preferred_element_type=F32)
        here = (hits > 0.0) & (rank == slot_left)
        mix_hi[pair] = jnp.where(here, high, 0.0).astype(BF)
        mix_lo[pair] = jnp.where(here, low, 0.0).astype(BF)
        placed = jnp.where(here, 1.0, 0.0).T.astype(BF)
        sent = jnp.dot(placed, both[:, :width], preferred_element_type=F32).astype(BF)
        outgoing[:, 2 * pair * slots:2 * (pair + 1) * slots, :] = sent.reshape(msgs, 2 * slots, width)

    def a_copy(i, dc):
        return remote(
            outgoing.at[2 * i + dc], arrived.at[2 * back[i] + c],
            s_a.at[2 * i + dc], r_a.at[2 * back[i] + c], along(order[i], c, (c + dc) % 2),
        )

    for i in range(ring):
        for dc in range(2):
            if i or dc:
                a_copy(i, dc).start()
    own_slots = pltpu.make_async_copy(outgoing.at[0], arrived.at[c], r_a.at[c])
    own_slots.start()

    def wait_in(buf, sem):
        pltpu.make_async_copy(buf, buf, sem).wait()

    def p_copy(k, step):
        p = (r + step) % planes
        return remote(psend.at[k, p], precv.at[k, step], s_p.at[k, step], r_p.at[k, step], x_peer(step))

    def h_copy(k, step):
        return remote(hid.at[k, r], hid.at[k, r], s_h.at[k, step], r_h.at[k, step], x_peer(step))

    def first(k):
        for m in range(planes):
            wait_in(arrived.at[planes * k + m], r_a.at[planes * k + m])
        x = arrived[planes * k:planes * (k + 1)].reshape(planes * msg_rows, width)
        for half in range(2):
            part = lax.dot_general(x, weights[half], (((1,), (1,)), ((), ())), preferred_element_type=F32)
            part = part.reshape(planes, msg_rows, hidden)
            pown[k, :, :, half * hidden:(half + 1) * hidden] = part
            psend[k, :, :, half * hidden:(half + 1) * hidden] = part.astype(BF)
        for step in range(1, planes):
            p_copy(k, step).start()

    def second(k):
        total = pown[k, r]
        for step in range(1, planes):
            p_copy(k, step).wait_recv()
            total = total + precv[k, step].astype(F32)
        g, u = total[:, :hidden], total[:, hidden:]
        hid[k, r] = (g / (1.0 + jnp.exp(-g)) * u).astype(BF)
        for step in range(1, planes):
            h_copy(k, step).start()

    def b_copy(m):
        i, s = m // 2, m % 2
        dc = (c + s) % 2
        return remote(
            outs.at[m], returned.at[2 * back[i] + dc], s_b.at[m], r_b.at[2 * back[i] + dc],
            along(order[i], s, s),
        )

    def third(k):
        for step in range(1, planes):
            p = (r + planes - step) % planes
            wait_in(hid.at[k, p], r_h.at[k, step])
        h = hid[k].reshape(planes * msg_rows, hidden)
        o = jnp.dot(h, down[...], preferred_element_type=F32).astype(BF)
        outs[planes * k:planes * (k + 1)] = o.reshape(planes, msg_rows, width)
        for m in range(planes * k, planes * (k + 1)):
            if m < 2:
                @pl.when(c != m)
                def _():
                    b_copy(m).start()

                @pl.when(c == m)
                def _():
                    pltpu.make_async_copy(outs.at[m], returned.at[0], r_b.at[0]).start()
            else:
                b_copy(m).start()

    own_gate.wait()
    own_up.wait()
    own_down.wait()
    for step in range(1, planes):
        for cp in w_copies(step):
            cp.wait_recv()
    chunks = msgs // planes
    for step in range(chunks + 2):
        if step < chunks:
            first(step)
        if 0 <= step - 1 < chunks:
            second(step - 1)
        if 0 <= step - 2 < chunks:
            third(step - 2)

    for jj in range(msgs):
        wait_in(returned.at[jj], r_b.at[jj])

    def z_copy(d):
        return remote(zsend.at[d], zrecv.at[(ring - d) % ring], s_z.at[d], r_z.at[d], along(d, 1 - c, c))

    for pair in range(ring // 2):
        got = returned[:, 2 * pair * slots:2 * (pair + 1) * slots, :].reshape(lanes, width)
        part = jnp.dot(mix_hi[pair], got, preferred_element_type=F32)
        part = part + jnp.dot(mix_lo[pair], got, preferred_element_type=F32)
        zsend[2 * pair:2 * pair + 2] = part.reshape(2, rows, width).astype(BF)
        for d in (2 * pair, 2 * pair + 1):
            if d:
                z_copy(d).start()

    total = zsend[0].astype(F32)
    for d in range(1, ring):
        z_copy(d).wait_recv()
        total = total + zrecv[(ring - d) % ring].astype(F32)
    fin[...] = total.astype(BF).reshape(planes, block, width)

    def f_copy(step):
        p = (r + step) % planes
        return remote(fin.at[p], cols.at[r], s_f.at[step], r_f.at[step], x_peer(step))

    for step in range(1, planes):
        f_copy(step).start()
    own_cols = pltpu.make_async_copy(fin.at[r], cols.at[r], l_sem.at[5])
    own_cols.start()
    own_cols.wait()
    for step in range(1, planes):
        p = (r + planes - step) % planes
        wait_in(cols.at[p], r_f.at[step])
    for p in range(planes):
        out_ref[:, p * width:(p + 1) * width] = cols[p]

    for step in range(1, planes):
        for cp in x_copies(step) + w_copies(step):
            cp.wait_send()
        f_copy(step).wait_send()
        for k in range(chunks):
            p_copy(k, step).wait_send()
            h_copy(k, step).wait_send()
    for d in range(1, ring):
        ag_copy(d).wait_send()
        z_copy(d).wait_send()
    for i in range(ring):
        for dc in range(2):
            if i or dc:
                a_copy(i, dc).wait_send()
    for m in range(msgs):
        if m < 2:
            @pl.when(c != m)
            def _():
                b_copy(m).wait_send()
        else:
            b_copy(m).wait_send()


def on_device(tokens, expert_ids, route_weights, gate_weight, up_weight, down_weight):
    block, top = expert_ids.shape
    planes = lax.axis_size("rep")
    ring = lax.axis_size("local")
    width = down_weight.shape[2]
    hidden = down_weight.shape[1]
    quarter = hidden // planes
    rows, slots, msgs = planes * block, planes * 2, 2 * ring
    msg_rows, chunks = ring * slots, 2 * ring // planes
    high = lax.reduce_precision(route_weights, exponent_bits=8, mantissa_bits=7)
    meta = jnp.concatenate(
        [expert_ids.astype(F32), high, route_weights - high, jnp.zeros((block, META - 3 * top), F32)], axis=1
    ).astype(BF)
    dma = pltpu.SemaphoreType.DMA
    return pl.pallas_call(
        functools.partial(kernel, (planes, ring, block, top, width, hidden)),
        out_shape=jax.ShapeDtypeStruct(tokens.shape, BF),
        in_specs=[pl.BlockSpec(memory_space=pltpu.VMEM)] * 2 + [pl.BlockSpec(memory_space=pl.ANY)] * 3,
        out_specs=pl.BlockSpec(memory_space=pltpu.VMEM),
        scratch_shapes=[
            pltpu.VMEM((ring, rows, width + META), BF),
            pltpu.VMEM((msgs, msg_rows, width), BF),
            pltpu.VMEM((msgs, msg_rows, width), BF),
            pltpu.VMEM((2, hidden, width), BF),
            pltpu.VMEM((hidden, width), BF),
            pltpu.VMEM((chunks, planes, msg_rows, 2 * hidden), BF),
            pltpu.VMEM((chunks, planes, msg_rows, 2 * hidden), F32),
            pltpu.VMEM((chunks, planes, msg_rows, 2 * hidden), BF),
            pltpu.VMEM((chunks, planes, msg_rows, hidden), BF),
            pltpu.VMEM((msgs, msg_rows, width), BF),
            pltpu.VMEM((msgs, msg_rows, width), BF),
            pltpu.VMEM((ring // 2, 2 * rows, msgs * 2 * slots), BF),
            pltpu.VMEM((ring // 2, 2 * rows, msgs * 2 * slots), BF),
            pltpu.VMEM((ring, rows, width), BF),
            pltpu.VMEM((ring, rows, width), BF),
            pltpu.VMEM((planes, block, width), BF),
            pltpu.VMEM((planes, block, width), BF),
        ]
        + [dma((planes,))] * 4
        + [dma((2, planes))] * 2
        + [dma((ring,))] * 2
        + [dma((msgs,))] * 2
        + [dma((chunks, planes))] * 4
        + [dma((msgs,))] * 2
        + [dma((ring,))] * 2
        + [dma((planes,))] * 2
        + [dma((6,))],
        compiler_params=pltpu.CompilerParams(
            collective_id=0, has_side_effects=True, vmem_limit_bytes=56 * 2**20
        ),
    )(tokens, meta, gate_weight, up_weight, down_weight)


def solution(mesh):
    placed = (
        P(("rep", "node", "local"), None),
        P(("rep", "node", "local"), None),
        P(("rep", "node", "local"), None),
        P(("node", "local"), "rep", None),
        P(("node", "local"), "rep", None),
        P(("node", "local"), None, "rep"),
    )
    return jax.shard_map(
        on_device,
        mesh=mesh,
        in_specs=placed,
        out_specs=P(("rep", "node", "local"), None),
        check_vma=False,
    )
```

```python
import functools

import jax
import jax.numpy as jnp
from jax import lax
from jax.experimental import pallas as pl
from jax.experimental.pallas import tpu as pltpu
from jax.sharding import PartitionSpec as P

MESH = pl.DeviceIdType.MESH
BF, F32 = jnp.bfloat16, jnp.float32
META = 128


def near_first(ring):
    order = [0]
    for step in range(1, ring // 2 + 1):
        order += [step] if 2 * step == ring else [step, ring - step]
    return order


def kernel(dims, tok_ref, ids_ref, share_ref, gate_ref, up_ref, down_ref, out_ref, *scratch):
    planes, ring, block, top, width, hidden = dims
    (
        meta_ref, rows_all, outgoing, arrived, weights, down, psend, pown, precv, hid, outs,
        returned, mix_hi, mix_lo, zsend, zrecv, fin, cols,
        s_x, r_x, s_m, r_m, s_w, r_w, s_ag, r_ag, s_a, r_a, s_p, r_p, s_h, r_h,
        s_b, r_b, s_z, r_z, s_f, r_f, l_sem,
    ) = scratch
    quarter = hidden // planes
    rows = planes * block
    slots = planes * 2
    msgs = 2 * ring
    group = 2 * slots
    chunks = ring // 2
    part_rows = msgs * group // planes
    order = near_first(ring)
    back = [order.index((ring - d) % ring) for d in order]

    r = lax.axis_index("rep")
    node = lax.axis_index("node")
    z = lax.axis_index("local")
    y, c = node // 2, node % 2

    def x_peer(step):
        return ((r + step) % planes, node, z)

    def along(step, role, core):
        yy = (y + step * (1 - role)) % ring
        zz = (z + step * role) % ring
        return (r, 2 * yy + core, zz)

    def remote(src, dst, send, recv, device):
        return pltpu.make_async_remote_copy(
            src_ref=src, dst_ref=dst, send_sem=send, recv_sem=recv,
            device_id=device, device_id_type=MESH,
        )

    def col(p):
        return pl.ds(pl.multiple_of(p * width, 128), width)

    def row16(p, n=block):
        return pl.ds(pl.multiple_of(p * n, 16), n)

    barrier = pltpu.get_barrier_semaphore()
    partners = [x_peer(s) for s in range(1, planes)]
    partners += [(r, 2 * y + (c + 1) % 2, z)]
    for d in range(1, ring):
        for core in range(2):
            partners += [along(d, 0, core), along(d, 1, core)]
    for p in partners:
        pl.semaphore_signal(barrier, inc=1, device_id=p, device_id_type=MESH)

    own = [
        pltpu.make_async_copy(tok_ref.at[:, col(r)], rows_all.at[0, row16(r), pl.ds(0, width)], l_sem.at[0]),
        pltpu.make_async_copy(gate_ref.at[0, :, col(r)], weights.at[0, row16(r, quarter), :], l_sem.at[2]),
        pltpu.make_async_copy(up_ref.at[0, :, col(r)], weights.at[1, row16(r, quarter), :], l_sem.at[3]),
        pltpu.make_async_copy(down_ref.at[0], down, l_sem.at[4]),
    ]
    for cp in own:
        cp.start()

    share = share_ref[...]
    high = share.astype(BF)
    low = (share - high.astype(F32)).astype(BF)
    k_of = lax.broadcasted_iota(jnp.int32, (top, META), 0)
    l_of = lax.broadcasted_iota(jnp.int32, (top, META), 1)
    meta_own = jnp.zeros((block, META), F32)
    for n, part in enumerate((ids_ref[...].astype(F32).astype(BF), high, low)):
        pick = jnp.where(l_of == k_of + n * top, 1.0, 0.0).astype(BF)
        meta_own += lax.dot_general(part, pick, (((0,), (0,)), ((), ())), preferred_element_type=F32)
    meta_ref[...] = meta_own.astype(BF)
    own_meta = pltpu.make_async_copy(meta_ref, rows_all.at[0, row16(r), pl.ds(width, META)], l_sem.at[1])
    own_meta.start()
    pl.semaphore_wait(barrier, len(partners))

    def x_copies(step):
        p = (r + step) % planes
        here = row16(r)
        return (
            remote(tok_ref.at[:, col(p)], rows_all.at[0, here, pl.ds(0, width)],
                   s_x.at[step], r_x.at[step], x_peer(step)),
            remote(meta_ref, rows_all.at[0, here, pl.ds(width, META)],
                   s_m.at[step], r_m.at[step], x_peer(step)),
        )

    for step in range(1, planes):
        for cp in x_copies(step):
            cp.start()
    own[0].wait()
    own_meta.wait()
    for step in range(1, planes):
        for cp in x_copies(step):
            cp.wait_recv()

    def ag_copy(i):
        return remote(rows_all.at[0], rows_all.at[back[i]], s_ag.at[i], r_ag.at[back[i]], along(order[i], 1 - c, c))

    for i in range(1, ring):
        ag_copy(i).start()

    def w_copies(step):
        p = (r + step) % planes
        here = row16(r, quarter)
        return (
            remote(gate_ref.at[0, :, col(p)], weights.at[0, here, :], s_w.at[0, step], r_w.at[0, step], x_peer(step)),
            remote(up_ref.at[0, :, col(p)], weights.at[1, here, :], s_w.at[1, step], r_w.at[1, step], x_peer(step)),
        )

    for step in range(1, planes):
        for cp in w_copies(step):
            cp.start()

    lanes = msgs * group
    shape = (2 * rows, lanes)
    t = lax.broadcasted_iota(jnp.int32, shape, 0)
    q = lax.broadcasted_iota(jnp.int32, shape, 1)
    j = q // group
    pos, dc = j // 2, j % 2
    d_of = jnp.where(pos % 2 == 1, (pos + 1) // 2, (ring - pos // 2) % ring)
    expert = (2 * ((y + d_of * (1 - c)) % ring) + (c + dc) % 2) * ring + (z + d_of * c) % ring
    expert = expert.astype(F32)
    same_block = (t // rows) == ((q // slots) % 2)
    expert = jnp.where(same_block, expert, -1.0)
    slot_left = ((q % slots) - 2 * ((t // block) % planes)).astype(F32)
    a = lax.broadcasted_iota(jnp.int32, (2 * rows, 2 * rows), 0)
    b = lax.broadcasted_iota(jnp.int32, (2 * rows, 2 * rows), 1)
    earlier = jnp.where((b < a) & (a // block == b // block), 1.0, 0.0).astype(BF)

    def a_copy(k, i, dc):
        return remote(
            outgoing.at[k, 2 * i + dc], arrived.at[k, 2 * back[i] + c],
            s_a.at[k, 2 * i + dc], r_a.at[k, 2 * back[i] + c], along(order[i], c, (c + dc) % 2),
        )

    def own_slots(k):
        return pltpu.make_async_copy(outgoing.at[k, 0], arrived.at[k, c], r_a.at[k, c])

    def place(k):
        for i in (2 * k, 2 * k + 1):
            if i:
                remote(rows_all.at[0], rows_all.at[i], s_ag.at[i], r_ag.at[i], x_peer(1)).wait_recv()
        both = rows_all[2 * k:2 * k + 2].reshape(2 * rows, width + META)
        meta = both[:, width:].astype(F32)
        hits = jnp.zeros(shape, F32)
        high = jnp.zeros(shape, F32)
        low = jnp.zeros(shape, F32)
        for n in range(top):
            named = meta[:, n:n + 1] == expert
            hits = jnp.where(named, 1.0, hits)
            high = jnp.where(named, meta[:, top + n:top + n + 1], high)
            low = jnp.where(named, meta[:, 2 * top + n:2 * top + n + 1], low)
        rank = jnp.dot(earlier, hits.astype(BF), preferred_element_type=F32)
        here = (hits > 0.0) & (rank == slot_left)
        mix_hi[k] = jnp.where(here, high, 0.0).astype(BF)
        mix_lo[k] = jnp.where(here, low, 0.0).astype(BF)
        placed = jnp.where(here, 1.0, 0.0).T.astype(BF)
        sent = jnp.dot(placed, both[:, :width], preferred_element_type=F32).astype(BF)
        outgoing[k] = sent.reshape(msgs, group, width)
        for i in range(ring):
            for dc in range(2):
                if i or dc:
                    a_copy(k, i, dc).start()
        own_slots(k).start()

    def wait_in(buf, sem):
        pltpu.make_async_copy(buf, buf, sem).wait()

    def p_copy(k, step):
        p = (r + step) % planes
        return remote(psend.at[k, p], precv.at[k, step], s_p.at[k, step], r_p.at[k, step], x_peer(step))

    def h_copy(k, step):
        return remote(hid.at[k, r], hid.at[k, r], s_h.at[k, step], r_h.at[k, step], x_peer(step))

    def first(k):
        for m in range(msgs):
            wait_in(arrived.at[k, m], r_a.at[k, m])
        x = arrived[k].reshape(msgs * group, width)
        for half in range(2):
            part = lax.dot_general(x, weights[half], (((1,), (1,)), ((), ())), preferred_element_type=F32)
            part = part.reshape(planes, part_rows, hidden)
            pown[k, :, :, half * hidden:(half + 1) * hidden] = part
            psend[k, :, :, half * hidden:(half + 1) * hidden] = part.astype(BF)
        for step in range(1, planes):
            p_copy(k, step).start()

    def second(k):
        total = pown[k, r]
        for step in range(1, planes):
            p_copy(k, step).wait_recv()
            total = total + precv[k, step].astype(F32)
        g, u = total[:, :hidden], total[:, hidden:]
        hid[k, r] = (g / (1.0 + jnp.exp(-g)) * u).astype(BF)
        for step in range(1, planes):
            h_copy(k, step).start()

    def b_copy(k, m):
        i, s = m // 2, m % 2
        dc = (c + s) % 2
        return remote(
            outs.at[k, m], returned.at[k, 2 * back[i] + dc], s_b.at[k, m], r_b.at[k, 2 * back[i] + dc],
            along(order[i], s, s),
        )

    def third(k):
        for step in range(1, planes):
            p = (r + planes - step) % planes
            wait_in(hid.at[k, p], r_h.at[k, step])
        h = hid[k].reshape(msgs * group, hidden)
        o = jnp.dot(h, down[...], preferred_element_type=F32).astype(BF)
        outs[k] = o.reshape(msgs, group, width)
        for m in range(msgs):
            if m < 2:
                @pl.when(c != m)
                def _():
                    b_copy(k, m).start()

                @pl.when(c == m)
                def _():
                    pltpu.make_async_copy(outs.at[k, m], returned.at[k, 0], r_b.at[k, 0]).start()
            else:
                b_copy(k, m).start()

    def z_copy(i):
        return remote(zsend.at[i], zrecv.at[back[i]], s_z.at[i], r_z.at[back[i]], along(order[i], 1 - c, c))

    def mix(k):
        for jj in range(msgs):
            wait_in(returned.at[k, jj], r_b.at[k, jj])
        got = returned[k].reshape(lanes, width)
        part = jnp.dot(mix_hi[k], got, preferred_element_type=F32)
        part = part + jnp.dot(mix_lo[k], got, preferred_element_type=F32)
        zsend[2 * k:2 * k + 2] = part.reshape(2, rows, width).astype(BF)
        for i in (2 * k, 2 * k + 1):
            if i:
                z_copy(i).start()

    for k in range(chunks):
        place(k)
    for cp in own[1:]:
        cp.wait()
    for step in range(1, planes):
        for cp in w_copies(step):
            cp.wait_recv()
    stages = []
    for k in range(chunks):
        stages += [(2 * k, 0, first, k), (2 * k + 3, 1, second, k), (2 * k + 6, 2, third, k), (2 * k + 9, 3, mix, k)]
    for _, _, stage, k in sorted(stages, key=lambda e: e[:2]):
        stage(k)

    total = zsend[0].astype(F32)
    for i in range(1, ring):
        wait_in(zrecv.at[i], r_z.at[i])
        total = total + zrecv[i].astype(F32)
    fin[...] = total.astype(BF).reshape(planes, block, width)

    def f_copy(step):
        p = (r + step) % planes
        return remote(fin.at[p], cols.at[r], s_f.at[step], r_f.at[step], x_peer(step))

    for step in range(1, planes):
        f_copy(step).start()
    own_cols = pltpu.make_async_copy(fin.at[r], cols.at[r], l_sem.at[5])
    own_cols.start()

    for step in range(1, planes):
        for cp in x_copies(step) + w_copies(step):
            cp.wait_send()
        for k in range(chunks):
            p_copy(k, step).wait_send()
            h_copy(k, step).wait_send()
    for i in range(1, ring):
        ag_copy(i).wait_send()
        z_copy(i).wait_send()
    for k in range(chunks):
        for i in range(ring):
            for dc in range(2):
                if i or dc:
                    a_copy(k, i, dc).wait_send()
        for m in range(msgs):
            if m < 2:
                @pl.when(c != m)
                def _():
                    b_copy(k, m).wait_send()
            else:
                b_copy(k, m).wait_send()

    own_cols.wait()
    for step in range(1, planes):
        wait_in(cols.at[(r + planes - step) % planes], r_f.at[step])
    for p in range(planes):
        out_ref[:, p * width:(p + 1) * width] = cols[p]
    for step in range(1, planes):
        f_copy(step).wait_send()


def on_device(tokens, expert_ids, route_weights, gate_weight, up_weight, down_weight):
    block, top = expert_ids.shape
    planes = lax.axis_size("rep")
    ring = lax.axis_size("local")
    width = down_weight.shape[2]
    hidden = down_weight.shape[1]
    rows, group, msgs = planes * block, planes * 4, 2 * ring
    chunks = ring // 2
    part_rows = msgs * group // planes
    dma = pltpu.SemaphoreType.DMA
    return pl.pallas_call(
        functools.partial(kernel, (planes, ring, block, top, width, hidden)),
        out_shape=jax.ShapeDtypeStruct(tokens.shape, BF),
        in_specs=[pl.BlockSpec(memory_space=pltpu.VMEM)] * 3 + [pl.BlockSpec(memory_space=pl.ANY)] * 3,
        out_specs=pl.BlockSpec(memory_space=pltpu.VMEM),
        scratch_shapes=[
            pltpu.VMEM((block, META), BF),
            pltpu.VMEM((ring, rows, width + META), BF),
            pltpu.VMEM((chunks, msgs, group, width), BF),
            pltpu.VMEM((chunks, msgs, group, width), BF),
            pltpu.VMEM((2, hidden, width), BF),
            pltpu.VMEM((hidden, width), BF),
            pltpu.VMEM((chunks, planes, part_rows, 2 * hidden), BF),
            pltpu.VMEM((chunks, planes, part_rows, 2 * hidden), F32),
            pltpu.VMEM((chunks, planes, part_rows, 2 * hidden), BF),
            pltpu.VMEM((chunks, planes, part_rows, hidden), BF),
            pltpu.VMEM((chunks, msgs, group, width), BF),
            pltpu.VMEM((chunks, msgs, group, width), BF),
            pltpu.VMEM((chunks, 2 * rows, msgs * group), BF),
            pltpu.VMEM((chunks, 2 * rows, msgs * group), BF),
            pltpu.VMEM((ring, rows, width), BF),
            pltpu.VMEM((ring, rows, width), BF),
            pltpu.VMEM((planes, block, width), BF),
            pltpu.VMEM((planes, block, width), BF),
        ]
        + [dma((planes,))] * 4
        + [dma((2, planes))] * 2
        + [dma((ring,))] * 2
        + [dma((chunks, msgs))] * 2
        + [dma((chunks, planes))] * 4
        + [dma((chunks, msgs))] * 2
        + [dma((ring,))] * 2
        + [dma((planes,))] * 2
        + [dma((6,))],
        compiler_params=pltpu.CompilerParams(
            collective_id=0, has_side_effects=True, vmem_limit_bytes=56 * 2**20
        ),
    )(tokens, expert_ids.T, route_weights.T, gate_weight, up_weight, down_weight)


def solution(mesh):
    placed = (
        P(("rep", "node", "local"), None),
        P(("rep", "node", "local"), None),
        P(("rep", "node", "local"), None),
        P(("node", "local"), "rep", None),
        P(("node", "local"), "rep", None),
        P(("node", "local"), None, "rep"),
    )
    return jax.shard_map(
        on_device,
        mesh=mesh,
        in_specs=placed,
        out_specs=P(("rep", "node", "local"), None),
        check_vma=False,
    )
```

```python
import functools

import jax
import jax.numpy as jnp
from jax import lax
from jax.experimental import pallas as pl
from jax.experimental.pallas import tpu as pltpu
from jax.sharding import PartitionSpec as P

MESH = pl.DeviceIdType.MESH
BF, F32 = jnp.bfloat16, jnp.float32
META = 128


def near_first(ring):
    order = [0]
    for step in range(1, ring // 2 + 1):
        order += [step] if 2 * step == ring else [step, ring - step]
    return order


def kernel(dims, tok_ref, ids_ref, share_ref, gate_ref, up_ref, down_ref, out_ref, *scratch):
    planes, ring, block, top, width, hidden = dims
    (
        meta_ref, rows_all, outgoing, arrived, weights, down, psend, pown, precv, fwd, frecv, hid, outs,
        returned, mix_hi, mix_lo, zsend, zrecv, fin, cols,
        s_x, r_x, s_m, r_m, s_w, r_w, s_ag, r_ag, s_a, r_a, s_p, r_p, s_q, r_q, s_h, r_h, s_g, r_g,
        s_b, r_b, s_z, r_z, s_f, r_f, l_sem,
    ) = scratch
    quarter = hidden // planes
    rows = planes * block
    slots = planes * 2
    msgs = 2 * ring
    group = 2 * slots
    chunks = ring // 2
    part_rows = msgs * group // planes
    order = near_first(ring)
    back = [order.index((ring - d) % ring) for d in order]

    r = lax.axis_index("rep")
    node = lax.axis_index("node")
    z = lax.axis_index("local")
    y, c = node // 2, node % 2

    def x_peer(step):
        return ((r + step) % planes, node, z)

    def along(step, role, core):
        yy = (y + step * (1 - role)) % ring
        zz = (z + step * role) % ring
        return (r, 2 * yy + core, zz)

    def remote(src, dst, send, recv, device):
        return pltpu.make_async_remote_copy(
            src_ref=src, dst_ref=dst, send_sem=send, recv_sem=recv,
            device_id=device, device_id_type=MESH,
        )

    def col(p):
        return pl.ds(pl.multiple_of(p * width, 128), width)

    def row16(p, n=block):
        return pl.ds(pl.multiple_of(p * n, 16), n)

    barrier = pltpu.get_barrier_semaphore()
    partners = [x_peer(s) for s in range(1, planes)]
    partners += [(r, 2 * y + (c + 1) % 2, z)]
    for d in range(1, ring):
        for core in range(2):
            partners += [along(d, 0, core), along(d, 1, core)]
    for p in partners:
        pl.semaphore_signal(barrier, inc=1, device_id=p, device_id_type=MESH)

    own = [
        pltpu.make_async_copy(tok_ref.at[:, col(r)], rows_all.at[0, row16(r), pl.ds(0, width)], l_sem.at[0]),
        pltpu.make_async_copy(gate_ref.at[0, :, col(r)], weights.at[0, row16(r, quarter), :], l_sem.at[2]),
        pltpu.make_async_copy(up_ref.at[0, :, col(r)], weights.at[1, row16(r, quarter), :], l_sem.at[3]),
        pltpu.make_async_copy(down_ref.at[0], down, l_sem.at[4]),
    ]
    for cp in own:
        cp.start()

    share = share_ref[...]
    high = share.astype(BF)
    low = (share - high.astype(F32)).astype(BF)
    k_of = lax.broadcasted_iota(jnp.int32, (top, META), 0)
    l_of = lax.broadcasted_iota(jnp.int32, (top, META), 1)
    meta_own = jnp.zeros((block, META), F32)
    for n, part in enumerate((ids_ref[...].astype(F32).astype(BF), high, low)):
        pick = jnp.where(l_of == k_of + n * top, 1.0, 0.0).astype(BF)
        meta_own += lax.dot_general(part, pick, (((0,), (0,)), ((), ())), preferred_element_type=F32)
    meta_ref[...] = meta_own.astype(BF)
    own_meta = pltpu.make_async_copy(meta_ref, rows_all.at[0, row16(r), pl.ds(width, META)], l_sem.at[1])
    own_meta.start()
    pl.semaphore_wait(barrier, len(partners))

    def x_copies(step):
        p = (r + step) % planes
        here = row16(r)
        return (
            remote(tok_ref.at[:, col(p)], rows_all.at[0, here, pl.ds(0, width)],
                   s_x.at[step], r_x.at[step], x_peer(step)),
            remote(meta_ref, rows_all.at[0, here, pl.ds(width, META)],
                   s_m.at[step], r_m.at[step], x_peer(step)),
        )

    for step in range(1, planes):
        for cp in x_copies(step):
            cp.start()
    own[0].wait()
    own_meta.wait()
    for step in range(1, planes):
        for cp in x_copies(step):
            cp.wait_recv()

    def ag_copy(i):
        return remote(rows_all.at[0], rows_all.at[back[i]], s_ag.at[i], r_ag.at[back[i]], along(order[i], 1 - c, c))

    for i in range(1, ring):
        ag_copy(i).start()

    def w_copies(step):
        p = (r + step) % planes
        here = row16(r, quarter)
        return (
            remote(gate_ref.at[0, :, col(p)], weights.at[0, here, :], s_w.at[0, step], r_w.at[0, step], x_peer(step)),
            remote(up_ref.at[0, :, col(p)], weights.at[1, here, :], s_w.at[1, step], r_w.at[1, step], x_peer(step)),
        )

    for step in range(1, planes):
        for cp in w_copies(step):
            cp.start()

    lanes = msgs * group
    shape = (2 * rows, lanes)
    t = lax.broadcasted_iota(jnp.int32, shape, 0)
    q = lax.broadcasted_iota(jnp.int32, shape, 1)
    j = q // group
    pos, dc = j // 2, j % 2
    d_of = jnp.where(pos % 2 == 1, (pos + 1) // 2, (ring - pos // 2) % ring)
    expert = (2 * ((y + d_of * (1 - c)) % ring) + (c + dc) % 2) * ring + (z + d_of * c) % ring
    expert = expert.astype(F32)
    same_block = (t // rows) == ((q // slots) % 2)
    expert = jnp.where(same_block, expert, -1.0)
    slot_left = ((q % slots) - 2 * ((t // block) % planes)).astype(F32)
    a = lax.broadcasted_iota(jnp.int32, (2 * rows, 2 * rows), 0)
    b = lax.broadcasted_iota(jnp.int32, (2 * rows, 2 * rows), 1)
    earlier = jnp.where((b < a) & (a // block == b // block), 1.0, 0.0).astype(BF)

    def a_copy(k, i, dc):
        return remote(
            outgoing.at[k, 2 * i + dc], arrived.at[k, 2 * back[i] + c],
            s_a.at[k, 2 * i + dc], r_a.at[k, 2 * back[i] + c], along(order[i], c, (c + dc) % 2),
        )

    def own_slots(k):
        return pltpu.make_async_copy(outgoing.at[k, 0], arrived.at[k, c], r_a.at[k, c])

    def place(k):
        for i in (2 * k, 2 * k + 1):
            if i:
                remote(rows_all.at[0], rows_all.at[i], s_ag.at[i], r_ag.at[i], x_peer(1)).wait_recv()
        both = rows_all[2 * k:2 * k + 2].reshape(2 * rows, width + META)
        meta = both[:, width:].astype(F32)
        hits = jnp.zeros(shape, F32)
        high = jnp.zeros(shape, F32)
        low = jnp.zeros(shape, F32)
        for n in range(top):
            named = meta[:, n:n + 1] == expert
            hits = jnp.where(named, 1.0, hits)
            high = jnp.where(named, meta[:, top + n:top + n + 1], high)
            low = jnp.where(named, meta[:, 2 * top + n:2 * top + n + 1], low)
        rank = jnp.dot(earlier, hits.astype(BF), preferred_element_type=F32)
        here = (hits > 0.0) & (rank == slot_left)
        mix_hi[k] = jnp.where(here, high, 0.0).astype(BF)
        mix_lo[k] = jnp.where(here, low, 0.0).astype(BF)
        placed = jnp.where(here, 1.0, 0.0).T.astype(BF)
        sent = jnp.dot(placed, both[:, :width], preferred_element_type=F32).astype(BF)
        outgoing[k] = sent.reshape(msgs, group, width)
        for i in range(ring):
            for dc in range(2):
                if i or dc:
                    a_copy(k, i, dc).start()
        own_slots(k).start()

    def wait_in(buf, sem):
        pltpu.make_async_copy(buf, buf, sem).wait()

    near = (r + 1 - 2 * (r % 2), planes - 1 - r)
    far = (r + 2) % planes

    def plane(p):
        return (p, node, z)

    def p_copy(k, half, n):
        to = near[half]
        return remote(psend.at[k, half, far if n else to], precv.at[k, half, n], s_p.at[k, half, n], r_p.at[k, half, n], plane(to))

    def q_copy(k, half):
        return remote(fwd.at[k, half], frecv.at[k, half], s_q.at[k, half], r_q.at[k, half], plane(near[1 - half]))

    def h_copy(k, n):
        return remote(hid.at[k, r], hid.at[k, r], s_h.at[k, n], r_h.at[k, n], plane(near[n]))

    def g_copy(k, n):
        part = hid.at[k, near[n], :, pl.ds(n * (hidden // 2), hidden // 2)]
        return remote(part, part, s_g.at[k, n], r_g.at[k, n], plane(near[1 - n]))

    def first(k):
        for m in range(msgs):
            wait_in(arrived.at[k, m], r_a.at[k, m])
        x = arrived[k].reshape(msgs * group, width)
        for half in range(2):
            part = lax.dot_general(x, weights[half], (((1,), (1,)), ((), ())), preferred_element_type=F32)
            part = part.reshape(planes, part_rows, hidden)
            pown[k, half] = part
            psend[k, half] = part.astype(BF)
            for n in (1, 0):
                p_copy(k, half, n).start()

    def pass_on(k):
        for half in range(2):
            p_copy(k, half, 1).wait_recv()
            fwd[k, half] = (pown[k, half, near[1 - half]] + precv[k, half, 1].astype(F32)).astype(BF)
            q_copy(k, half).start()

    def second(k):
        sums = []
        for half in range(2):
            p_copy(k, half, 0).wait_recv()
            q_copy(k, half).wait_recv()
            sums.append(pown[k, half, r] + precv[k, half, 0].astype(F32) + frecv[k, half].astype(F32))
        g, u = sums
        hid[k, r] = (g / (1.0 + jnp.exp(-g)) * u).astype(BF)
        for n in range(2):
            h_copy(k, n).start()

    def relay(k):
        for n in range(2):
            wait_in(hid.at[k, near[n]], r_h.at[k, n])
            g_copy(k, n).start()

    def b_copy(k, m):
        i, s = m // 2, m % 2
        dc = (c + s) % 2
        return remote(
            outs.at[k, m], returned.at[k, 2 * back[i] + dc], s_b.at[k, m], r_b.at[k, 2 * back[i] + dc],
            along(order[i], s, s),
        )

    def third(k):
        for n in range(2):
            wait_in(hid.at[k, far, :, pl.ds(n * (hidden // 2), hidden // 2)], r_g.at[k, n])
        h = hid[k].reshape(msgs * group, hidden)
        o = jnp.dot(h, down[...], preferred_element_type=F32).astype(BF)
        outs[k] = o.reshape(msgs, group, width)
        for m in range(msgs):
            if m < 2:
                @pl.when(c != m)
                def _():
                    b_copy(k, m).start()

                @pl.when(c == m)
                def _():
                    pltpu.make_async_copy(outs.at[k, m], returned.at[k, 0], r_b.at[k, 0]).start()
            else:
                b_copy(k, m).start()

    def z_copy(i):
        return remote(zsend.at[i], zrecv.at[back[i]], s_z.at[i], r_z.at[back[i]], along(order[i], 1 - c, c))

    def mix(k):
        for jj in range(msgs):
            wait_in(returned.at[k, jj], r_b.at[k, jj])
        got = returned[k].reshape(lanes, width)
        part = jnp.dot(mix_hi[k], got, preferred_element_type=F32)
        part = part + jnp.dot(mix_lo[k], got, preferred_element_type=F32)
        zsend[2 * k:2 * k + 2] = part.reshape(2, rows, width).astype(BF)
        for i in (2 * k, 2 * k + 1):
            if i:
                z_copy(i).start()

    for k in range(chunks):
        place(k)
    for cp in own[1:]:
        cp.wait()
    for step in range(1, planes):
        for cp in w_copies(step):
            cp.wait_recv()
    stages = []
    for n, k in enumerate([*range(1, chunks), 0]):
        for depth, (late, stage) in enumerate(((0, first), (4, pass_on), (7, second), (10, relay), (13, third), (17, mix))):
            stages.append((3 * n + late, -depth, stage, k))
    for _, _, stage, k in sorted(stages, key=lambda e: e[:2]):
        stage(k)

    total = zsend[0].astype(F32)
    for i in range(1, ring):
        wait_in(zrecv.at[i], r_z.at[i])
        total = total + zrecv[i].astype(F32)
    fin[...] = total.astype(BF).reshape(planes, block, width)

    def f_copy(step):
        p = (r + step) % planes
        return remote(fin.at[p], cols.at[r], s_f.at[step], r_f.at[step], x_peer(step))

    for step in range(1, planes):
        f_copy(step).start()
    own_cols = pltpu.make_async_copy(fin.at[r], cols.at[r], l_sem.at[5])
    own_cols.start()

    for step in range(1, planes):
        for cp in x_copies(step) + w_copies(step):
            cp.wait_send()
    for i in range(1, ring):
        ag_copy(i).wait_send()
        z_copy(i).wait_send()
    for k in range(chunks):
        for n in range(2):
            p_copy(k, n, 0).wait_send()
            p_copy(k, n, 1).wait_send()
            q_copy(k, n).wait_send()
            h_copy(k, n).wait_send()
            g_copy(k, n).wait_send()
        for i in range(ring):
            for dc in range(2):
                if i or dc:
                    a_copy(k, i, dc).wait_send()
        for m in range(msgs):
            if m < 2:
                @pl.when(c != m)
                def _():
                    b_copy(k, m).wait_send()
            else:
                b_copy(k, m).wait_send()

    own_cols.wait()
    for step in range(1, planes):
        wait_in(cols.at[(r + planes - step) % planes], r_f.at[step])
    for p in range(planes):
        out_ref[:, p * width:(p + 1) * width] = cols[p]
    for step in range(1, planes):
        f_copy(step).wait_send()


def on_device(tokens, expert_ids, route_weights, gate_weight, up_weight, down_weight):
    block, top = expert_ids.shape
    planes = lax.axis_size("rep")
    ring = lax.axis_size("local")
    width = down_weight.shape[2]
    hidden = down_weight.shape[1]
    rows, group, msgs = planes * block, planes * 4, 2 * ring
    chunks = ring // 2
    part_rows = msgs * group // planes
    dma = pltpu.SemaphoreType.DMA
    return pl.pallas_call(
        functools.partial(kernel, (planes, ring, block, top, width, hidden)),
        out_shape=jax.ShapeDtypeStruct(tokens.shape, BF),
        in_specs=[pl.BlockSpec(memory_space=pltpu.VMEM)] * 3 + [pl.BlockSpec(memory_space=pl.ANY)] * 3,
        out_specs=pl.BlockSpec(memory_space=pltpu.VMEM),
        scratch_shapes=[
            pltpu.VMEM((block, META), BF),
            pltpu.VMEM((ring, rows, width + META), BF),
            pltpu.VMEM((chunks, msgs, group, width), BF),
            pltpu.VMEM((chunks, msgs, group, width), BF),
            pltpu.VMEM((2, hidden, width), BF),
            pltpu.VMEM((hidden, width), BF),
            pltpu.VMEM((chunks, 2, planes, part_rows, hidden), BF),
            pltpu.VMEM((chunks, 2, planes, part_rows, hidden), F32),
            pltpu.VMEM((chunks, 2, 2, part_rows, hidden), BF),
            pltpu.VMEM((chunks, 2, part_rows, hidden), BF),
            pltpu.VMEM((chunks, 2, part_rows, hidden), BF),
            pltpu.VMEM((chunks, planes, part_rows, hidden), BF),
            pltpu.VMEM((chunks, msgs, group, width), BF),
            pltpu.VMEM((chunks, msgs, group, width), BF),
            pltpu.VMEM((chunks, 2 * rows, msgs * group), BF),
            pltpu.VMEM((chunks, 2 * rows, msgs * group), BF),
            pltpu.VMEM((ring, rows, width), BF),
            pltpu.VMEM((ring, rows, width), BF),
            pltpu.VMEM((planes, block, width), BF),
            pltpu.VMEM((planes, block, width), BF),
        ]
        + [dma((planes,))] * 4
        + [dma((2, planes))] * 2
        + [dma((ring,))] * 2
        + [dma((chunks, msgs))] * 2
        + [dma((chunks, 2, 2))] * 2
        + [dma((chunks, 2))] * 6
        + [dma((chunks, msgs))] * 2
        + [dma((ring,))] * 2
        + [dma((planes,))] * 2
        + [dma((6,))],
        compiler_params=pltpu.CompilerParams(
            collective_id=0, has_side_effects=True, vmem_limit_bytes=56 * 2**20
        ),
    )(tokens, expert_ids.T, route_weights.T, gate_weight, up_weight, down_weight)


def solution(mesh):
    placed = (
        P(("rep", "node", "local"), None),
        P(("rep", "node", "local"), None),
        P(("rep", "node", "local"), None),
        P(("node", "local"), "rep", None),
        P(("node", "local"), "rep", None),
        P(("node", "local"), None, "rep"),
    )
    return jax.shard_map(
        on_device,
        mesh=mesh,
        in_specs=placed,
        out_specs=P(("rep", "node", "local"), None),
        check_vma=False,
    )
```

```python
import functools

import jax
import jax.numpy as jnp
from jax import lax
from jax.experimental import pallas as pl
from jax.experimental.pallas import tpu as pltpu
from jax.sharding import PartitionSpec as P

MESH = pl.DeviceIdType.MESH
BF, F32 = jnp.bfloat16, jnp.float32
META = 128


def near_first(ring):
    order = [0]
    for step in range(1, ring // 2 + 1):
        order += [step] if 2 * step == ring else [step, ring - step]
    return order


def kernel(dims, tok_ref, ids_ref, share_ref, gate_ref, up_ref, down_ref, out_ref, *scratch):
    planes, ring, block, top, width, hidden = dims
    (
        meta_ref, rows_all, outgoing, arrived, weights, down, psend, pown, precv, fwd, frecv, hid, outs,
        returned, mix_hi, mix_lo, zsend, zrecv, fin, cols,
        s_x, r_x, s_m, r_m, s_w, r_w, s_ag, r_ag, s_a, r_a, s_p, r_p, s_q, r_q, s_h, r_h, s_g, r_g,
        s_b, r_b, s_z, r_z, s_f, r_f, l_sem,
    ) = scratch
    quarter = hidden // planes
    rows = planes * block
    slots = planes * 2
    msgs = 2 * ring
    group = 2 * slots
    chunks = ring // 2
    part_rows = msgs * group // planes
    order = near_first(ring)
    back = [order.index((ring - d) % ring) for d in order]

    r = lax.axis_index("rep")
    node = lax.axis_index("node")
    z = lax.axis_index("local")
    y, c = node // 2, node % 2

    def x_peer(step):
        return ((r + step) % planes, node, z)

    def along(step, role, core):
        yy = (y + step * (1 - role)) % ring
        zz = (z + step * role) % ring
        return (r, 2 * yy + core, zz)

    def remote(src, dst, send, recv, device):
        return pltpu.make_async_remote_copy(
            src_ref=src, dst_ref=dst, send_sem=send, recv_sem=recv,
            device_id=device, device_id_type=MESH,
        )

    def wait_in(buf, sem):
        pltpu.make_async_copy(buf, buf, sem).wait()

    def col(p):
        return pl.ds(pl.multiple_of(p * width, 128), width)

    def row16(p, n=block):
        return pl.ds(pl.multiple_of(p * n, 16), n)

    barrier = pltpu.get_barrier_semaphore()
    partners = [x_peer(s) for s in range(1, planes)]
    partners += [(r, 2 * y + (c + 1) % 2, z)]
    for d in range(1, ring):
        for core in range(2):
            partners += [along(d, 0, core), along(d, 1, core)]
    for p in partners:
        pl.semaphore_signal(barrier, inc=1, device_id=p, device_id_type=MESH)

    own = [
        pltpu.make_async_copy(tok_ref.at[:, col(r)], rows_all.at[0, row16(r), pl.ds(0, width)], l_sem.at[0]),
        pltpu.make_async_copy(gate_ref.at[0, :, col(r)], weights.at[0, row16(r, quarter), :], l_sem.at[2]),
        pltpu.make_async_copy(up_ref.at[0, :, col(r)], weights.at[1, row16(r, quarter), :], l_sem.at[3]),
        pltpu.make_async_copy(down_ref.at[0], down, l_sem.at[4]),
    ]
    for cp in own:
        cp.start()

    share = share_ref[...]
    high = share.astype(BF)
    low = (share - high.astype(F32)).astype(BF)
    k_of = lax.broadcasted_iota(jnp.int32, (top, META), 0)
    l_of = lax.broadcasted_iota(jnp.int32, (top, META), 1)
    meta_own = jnp.zeros((block, META), F32)
    for n, part in enumerate((ids_ref[...].astype(F32).astype(BF), high, low)):
        pick = jnp.where(l_of == k_of + n * top, 1.0, 0.0).astype(BF)
        meta_own += lax.dot_general(part, pick, (((0,), (0,)), ((), ())), preferred_element_type=F32)
    meta_ref[...] = meta_own.astype(BF)
    own_meta = pltpu.make_async_copy(meta_ref, rows_all.at[0, row16(r), pl.ds(width, META)], l_sem.at[1])
    own_meta.start()
    pl.semaphore_wait(barrier, len(partners))

    def x_copies(step):
        p = (r + step) % planes
        here = row16(r)
        return (
            remote(tok_ref.at[:, col(p)], rows_all.at[0, here, pl.ds(0, width)],
                   s_x.at[step], r_x.at[step], x_peer(step)),
            remote(meta_ref, rows_all.at[0, here, pl.ds(width, META)],
                   s_m.at[step], r_m.at[step], x_peer(step)),
        )

    for step in range(1, planes):
        for cp in x_copies(step):
            cp.start()
    own[0].wait()
    own_meta.wait()
    for step in range(1, planes):
        for cp in x_copies(step):
            cp.wait_recv()

    reach = ring // 4 or ring
    direct = [i for i in range(1, ring) if min(order[i], ring - order[i]) <= reach]
    relays = [(sign, e) for sign in (1, -1) for e in range(1, reach + 1) if reach < ring]
    opposite = order.index(ring // 2)

    def ag_copy(i):
        return remote(rows_all.at[0], rows_all.at[back[i]], s_ag.at[i], r_ag.at[back[i]], along(order[i], 1 - c, c))

    def on_copy(sign, e):
        source, there = order.index(-sign * reach % ring), order.index(-sign * (reach + e) % ring)
        part = pl.ds(0, rows)
        if there == opposite:
            part = pl.ds(0 if sign > 0 else rows // 2, rows // 2)
        return remote(
            rows_all.at[source, part, :], rows_all.at[there, part, :], s_ag.at[ring + relays.index((sign, e))],
            r_ag.at[ring if there == opposite and sign < 0 else there], along(sign * e % ring, 1 - c, c),
        )

    for i in direct:
        ag_copy(i).start()

    def w_copies(step):
        p = (r + step) % planes
        here = row16(r, quarter)
        return (
            remote(gate_ref.at[0, :, col(p)], weights.at[0, here, :], s_w.at[0, step], r_w.at[0, step], x_peer(step)),
            remote(up_ref.at[0, :, col(p)], weights.at[1, here, :], s_w.at[1, step], r_w.at[1, step], x_peer(step)),
        )

    for step in range(1, planes):
        for cp in w_copies(step):
            cp.start()

    lanes = msgs * group
    shape = (2 * rows, lanes)
    t = lax.broadcasted_iota(jnp.int32, shape, 0)
    q = lax.broadcasted_iota(jnp.int32, shape, 1)
    j = q // group
    pos, dc = j // 2, j % 2
    d_of = jnp.where(pos % 2 == 1, (pos + 1) // 2, (ring - pos // 2) % ring)
    expert = (2 * ((y + d_of * (1 - c)) % ring) + (c + dc) % 2) * ring + (z + d_of * c) % ring
    expert = expert.astype(F32)
    same_block = (t // rows) == ((q // slots) % 2)
    expert = jnp.where(same_block, expert, -1.0)
    slot_left = ((q % slots) - 2 * ((t // block) % planes)).astype(F32)
    a = lax.broadcasted_iota(jnp.int32, (2 * rows, 2 * rows), 0)
    b = lax.broadcasted_iota(jnp.int32, (2 * rows, 2 * rows), 1)
    earlier = jnp.where((b < a) & (a // block == b // block), 1.0, 0.0).astype(BF)

    def a_copy(k, i, dc):
        return remote(
            outgoing.at[k, 2 * i + dc], arrived.at[k, 2 * back[i] + c],
            s_a.at[k, 2 * i + dc], r_a.at[k, 2 * back[i] + c], along(order[i], c, (c + dc) % 2),
        )

    def own_slots(k):
        return pltpu.make_async_copy(outgoing.at[k, 0], arrived.at[k, c], r_a.at[k, c])

    def place(k):
        for i in (2 * k, 2 * k + 1):
            if i and i not in direct:
                if i == opposite:
                    wait_in(rows_all.at[i, pl.ds(0, rows // 2), :], r_ag.at[i])
                    wait_in(rows_all.at[i, pl.ds(rows // 2, rows // 2), :], r_ag.at[ring])
                else:
                    wait_in(rows_all.at[i], r_ag.at[i])
        both = rows_all[2 * k:2 * k + 2].reshape(2 * rows, width + META)
        meta = both[:, width:].astype(F32)
        hits = jnp.zeros(shape, F32)
        high = jnp.zeros(shape, F32)
        low = jnp.zeros(shape, F32)
        for n in range(top):
            named = meta[:, n:n + 1] == expert
            hits = jnp.where(named, 1.0, hits)
            high = jnp.where(named, meta[:, top + n:top + n + 1], high)
            low = jnp.where(named, meta[:, 2 * top + n:2 * top + n + 1], low)
        rank = jnp.dot(earlier, hits.astype(BF), preferred_element_type=F32)
        here = (hits > 0.0) & (rank == slot_left)
        mix_hi[k] = jnp.where(here, high, 0.0).astype(BF)
        mix_lo[k] = jnp.where(here, low, 0.0).astype(BF)
        placed = jnp.where(here, 1.0, 0.0).T.astype(BF)
        sent = jnp.dot(placed, both[:, :width], preferred_element_type=F32).astype(BF)
        outgoing[k] = sent.reshape(msgs, group, width)
        for i in range(ring):
            for dc in range(2):
                if i or dc:
                    a_copy(k, i, dc).start()
        own_slots(k).start()

    near = (r + 1 - 2 * (r % 2), planes - 1 - r)
    far = (r + 2) % planes

    def plane(p):
        return (p, node, z)

    def p_copy(k, half, n):
        to = near[half]
        return remote(psend.at[k, half, far if n else to], precv.at[k, half, n], s_p.at[k, half, n], r_p.at[k, half, n], plane(to))

    def q_copy(k, half):
        return remote(fwd.at[k, half], frecv.at[k, half], s_q.at[k, half], r_q.at[k, half], plane(near[1 - half]))

    def h_copy(k, n):
        return remote(hid.at[k, r], hid.at[k, r], s_h.at[k, n], r_h.at[k, n], plane(near[n]))

    def g_copy(k, n):
        part = hid.at[k, near[n], :, pl.ds(n * (hidden // 2), hidden // 2)]
        return remote(part, part, s_g.at[k, n], r_g.at[k, n], plane(near[1 - n]))

    def first(k):
        for m in range(msgs):
            wait_in(arrived.at[k, m], r_a.at[k, m])
        x = arrived[k].reshape(msgs * group, width)
        for half in range(2):
            part = lax.dot_general(x, weights[half], (((1,), (1,)), ((), ())), preferred_element_type=F32)
            part = part.reshape(planes, part_rows, hidden)
            pown[k, half] = part
            psend[k, half] = part.astype(BF)
            for n in (1, 0):
                p_copy(k, half, n).start()

    def pass_on(k):
        for i in range(ring):
            for dc in range(2):
                if i or dc:
                    a_copy(k, i, dc).wait_send()
        for half in range(2):
            p_copy(k, half, 1).wait_recv()
            fwd[k, half] = (pown[k, half, near[1 - half]] + precv[k, half, 1].astype(F32)).astype(BF)
            q_copy(k, half).start()

    def second(k):
        sums = []
        for half in range(2):
            p_copy(k, half, 0).wait_recv()
            q_copy(k, half).wait_recv()
            sums.append(pown[k, half, r] + precv[k, half, 0].astype(F32) + frecv[k, half].astype(F32))
        g, u = sums
        hid[k, r] = (g / (1.0 + jnp.exp(-g)) * u).astype(BF)
        for n in range(2):
            h_copy(k, n).start()

    def relay(k):
        for n in range(2):
            wait_in(hid.at[k, near[n]], r_h.at[k, n])
            g_copy(k, n).start()

    def b_copy(k, m):
        i, s = m // 2, m % 2
        dc = (c + s) % 2
        return remote(
            outs.at[k, m], returned.at[k, 2 * back[i] + dc], s_b.at[k, m], r_b.at[k, 2 * back[i] + dc],
            along(order[i], s, s),
        )

    def third(k):
        for n in range(2):
            wait_in(hid.at[k, far, :, pl.ds(n * (hidden // 2), hidden // 2)], r_g.at[k, n])
        h = hid[k].reshape(msgs * group, hidden)
        o = jnp.dot(h, down[...], preferred_element_type=F32).astype(BF)
        outs[k] = o.reshape(msgs, group, width)
        for m in range(msgs):
            if m < 2:
                @pl.when(c != m)
                def _():
                    b_copy(k, m).start()

                @pl.when(c == m)
                def _():
                    pltpu.make_async_copy(outs.at[k, m], returned.at[k, 0], r_b.at[k, 0]).start()
            else:
                b_copy(k, m).start()

    def z_copy(i):
        return remote(zsend.at[i], zrecv.at[back[i]], s_z.at[i], r_z.at[back[i]], along(order[i], 1 - c, c))

    def back_sent(k):
        for m in range(msgs):
            if m < 2:
                @pl.when(c != m)
                def _():
                    b_copy(k, m).wait_send()
            else:
                b_copy(k, m).wait_send()

    def mix(k):
        for n in range(2):
            p_copy(k, n, 0).wait_send()
            p_copy(k, n, 1).wait_send()
            q_copy(k, n).wait_send()
            h_copy(k, n).wait_send()
            g_copy(k, n).wait_send()
        if k != turns[0]:
            back_sent(turns[turns.index(k) - 1])
        for jj in range(msgs):
            wait_in(returned.at[k, jj], r_b.at[k, jj])
        got = returned[k].reshape(lanes, width)
        part = jnp.dot(mix_hi[k], got, preferred_element_type=F32)
        part = part + jnp.dot(mix_lo[k], got, preferred_element_type=F32)
        zsend[2 * k:2 * k + 2] = part.reshape(2, rows, width).astype(BF)
        for i in (2 * k, 2 * k + 1):
            if i:
                z_copy(i).start()

    turns = [*range(1, chunks), 0]
    for i in direct:
        wait_in(rows_all.at[i], r_ag.at[i])
    for sign, e in relays:
        on_copy(sign, e).start()
    for k in turns:
        place(k)
    for cp in own[1:]:
        cp.wait()
    for step in range(1, planes):
        for cp in w_copies(step):
            cp.wait_recv()
    stages = []
    for n, k in enumerate(turns):
        for depth, (late, stage) in enumerate(((-30 - 2 * n, first), (10, pass_on), (14, second), (18, relay), (22, third), (29, mix))):
            stages.append((3 * n + late, -depth, stage, k))
    for _, _, stage, k in sorted(stages, key=lambda e: e[:2]):
        stage(k)

    total = zsend[0].astype(F32)
    for i in range(1, ring):
        wait_in(zrecv.at[i], r_z.at[i])
        total = total + zrecv[i].astype(F32)
    fin[...] = total.astype(BF).reshape(planes, block, width)

    def f_copy(step):
        p = (r + step) % planes
        return remote(fin.at[p], cols.at[r], s_f.at[step], r_f.at[step], x_peer(step))

    for step in range(1, planes):
        f_copy(step).start()
    own_cols = pltpu.make_async_copy(fin.at[r], cols.at[r], l_sem.at[5])
    own_cols.start()

    for step in range(1, planes):
        for cp in x_copies(step) + w_copies(step):
            cp.wait_send()
    for i in direct:
        ag_copy(i).wait_send()
    for sign, e in relays:
        on_copy(sign, e).wait_send()
    for i in range(1, ring):
        z_copy(i).wait_send()
    back_sent(turns[-1])

    own_cols.wait()
    for step in range(1, planes):
        wait_in(cols.at[(r + planes - step) % planes], r_f.at[step])
    for p in range(planes):
        out_ref[:, p * width:(p + 1) * width] = cols[p]
    for step in range(1, planes):
        f_copy(step).wait_send()


def on_device(tokens, expert_ids, route_weights, gate_weight, up_weight, down_weight):
    block, top = expert_ids.shape
    planes = lax.axis_size("rep")
    ring = lax.axis_size("local")
    width = down_weight.shape[2]
    hidden = down_weight.shape[1]
    rows, group, msgs = planes * block, planes * 4, 2 * ring
    chunks = ring // 2
    part_rows = msgs * group // planes
    dma = pltpu.SemaphoreType.DMA
    return pl.pallas_call(
        functools.partial(kernel, (planes, ring, block, top, width, hidden)),
        out_shape=jax.ShapeDtypeStruct(tokens.shape, BF),
        in_specs=[pl.BlockSpec(memory_space=pltpu.VMEM)] * 3 + [pl.BlockSpec(memory_space=pl.ANY)] * 3,
        out_specs=pl.BlockSpec(memory_space=pltpu.VMEM),
        scratch_shapes=[
            pltpu.VMEM((block, META), BF),
            pltpu.VMEM((ring, rows, width + META), BF),
            pltpu.VMEM((chunks, msgs, group, width), BF),
            pltpu.VMEM((chunks, msgs, group, width), BF),
            pltpu.VMEM((2, hidden, width), BF),
            pltpu.VMEM((hidden, width), BF),
            pltpu.VMEM((chunks, 2, planes, part_rows, hidden), BF),
            pltpu.VMEM((chunks, 2, planes, part_rows, hidden), F32),
            pltpu.VMEM((chunks, 2, 2, part_rows, hidden), BF),
            pltpu.VMEM((chunks, 2, part_rows, hidden), BF),
            pltpu.VMEM((chunks, 2, part_rows, hidden), BF),
            pltpu.VMEM((chunks, planes, part_rows, hidden), BF),
            pltpu.VMEM((chunks, msgs, group, width), BF),
            pltpu.VMEM((chunks, msgs, group, width), BF),
            pltpu.VMEM((chunks, 2 * rows, msgs * group), BF),
            pltpu.VMEM((chunks, 2 * rows, msgs * group), BF),
            pltpu.VMEM((ring, rows, width), BF),
            pltpu.VMEM((ring, rows, width), BF),
            pltpu.VMEM((planes, block, width), BF),
            pltpu.VMEM((planes, block, width), BF),
        ]
        + [dma((planes,))] * 4
        + [dma((2, planes))] * 2
        + [dma((2 * ring,)), dma((ring + 1,))]
        + [dma((chunks, msgs))] * 2
        + [dma((chunks, 2, 2))] * 2
        + [dma((chunks, 2))] * 6
        + [dma((chunks, msgs))] * 2
        + [dma((ring,))] * 2
        + [dma((planes,))] * 2
        + [dma((6,))],
        compiler_params=pltpu.CompilerParams(
            collective_id=0, has_side_effects=True, vmem_limit_bytes=56 * 2**20
        ),
    )(tokens, expert_ids.T, route_weights.T, gate_weight, up_weight, down_weight)


def solution(mesh):
    placed = (
        P(("rep", "node", "local"), None),
        P(("rep", "node", "local"), None),
        P(("rep", "node", "local"), None),
        P(("node", "local"), "rep", None),
        P(("node", "local"), "rep", None),
        P(("node", "local"), None, "rep"),
    )
    return jax.shard_map(
        on_device,
        mesh=mesh,
        in_specs=placed,
        out_specs=P(("rep", "node", "local"), None),
        check_vma=False,
    )
```

```python
import functools

import jax
import jax.numpy as jnp
from jax import lax
from jax.experimental import pallas as pl
from jax.experimental.pallas import tpu as pltpu
from jax.sharding import PartitionSpec as P

MESH = pl.DeviceIdType.MESH
BF, F32 = jnp.bfloat16, jnp.float32
META = 128


def near_first(ring):
    order = [0]
    for step in range(1, ring // 2 + 1):
        order += [step] if 2 * step == ring else [step, ring - step]
    return order


def kernel(dims, tok_ref, ids_ref, share_ref, gate_ref, up_ref, down_ref, out_ref, *scratch):
    planes, ring, block, top, width, hidden = dims
    (
        meta_ref, rows_all, outgoing, arrived, weights, down, psend, pown, precv, fwd, frecv, hid, outs,
        returned, mix_hi, mix_lo, zsend, zrecv, fin, tsum,
        s_x, r_x, s_m, r_m, s_w, r_w, s_ag, r_ag, s_a, r_a, s_p, r_p, s_q, r_q, s_h, r_h, s_g, r_g,
        s_b, r_b, s_z, r_z, s_f, r_f, l_sem,
    ) = scratch
    quarter = hidden // planes
    rows = planes * block
    slots = planes * 2
    msgs = 2 * ring
    group = 2 * slots
    chunks = ring // 2
    part_rows = msgs * group // planes
    order = near_first(ring)
    back = [order.index((ring - d) % ring) for d in order]

    r = lax.axis_index("rep")
    node = lax.axis_index("node")
    z = lax.axis_index("local")
    y, c = node // 2, node % 2

    def x_peer(step):
        return ((r + step) % planes, node, z)

    def along(step, role, core):
        yy = (y + step * (1 - role)) % ring
        zz = (z + step * role) % ring
        return (r, 2 * yy + core, zz)

    def remote(src, dst, send, recv, device):
        return pltpu.make_async_remote_copy(
            src_ref=src, dst_ref=dst, send_sem=send, recv_sem=recv,
            device_id=device, device_id_type=MESH,
        )

    def col(p):
        return pl.ds(pl.multiple_of(p * width, 128), width)

    def row16(p, n=block):
        return pl.ds(pl.multiple_of(p * n, 16), n)

    barrier = pltpu.get_barrier_semaphore()
    partners = [x_peer(s) for s in range(1, planes)]
    partners += [(r, 2 * y + (c + 1) % 2, z)]
    for d in range(1, ring):
        for core in range(2):
            partners += [along(d, 0, core), along(d, 1, core)]
    for p in partners:
        pl.semaphore_signal(barrier, inc=1, device_id=p, device_id_type=MESH)

    own = [
        pltpu.make_async_copy(tok_ref.at[:, col(r)], rows_all.at[0, row16(r), pl.ds(0, width)], l_sem.at[0]),
        pltpu.make_async_copy(gate_ref.at[0, :, col(r)], weights.at[0, row16(r, quarter), :], l_sem.at[2]),
        pltpu.make_async_copy(up_ref.at[0, :, col(r)], weights.at[1, row16(r, quarter), :], l_sem.at[3]),
        pltpu.make_async_copy(down_ref.at[0], down, l_sem.at[4]),
    ]
    for cp in own:
        cp.start()

    share = share_ref[...]
    high = share.astype(BF)
    low = (share - high.astype(F32)).astype(BF)
    k_of = lax.broadcasted_iota(jnp.int32, (top, META), 0)
    l_of = lax.broadcasted_iota(jnp.int32, (top, META), 1)
    meta_own = jnp.zeros((block, META), F32)
    for n, part in enumerate((ids_ref[...].astype(F32).astype(BF), high, low)):
        pick = jnp.where(l_of == k_of + n * top, 1.0, 0.0).astype(BF)
        meta_own += lax.dot_general(part, pick, (((0,), (0,)), ((), ())), preferred_element_type=F32)
    meta_ref[...] = meta_own.astype(BF)
    own_meta = pltpu.make_async_copy(meta_ref, rows_all.at[0, row16(r), pl.ds(width, META)], l_sem.at[1])
    own_meta.start()
    pl.semaphore_wait(barrier, len(partners))

    def x_copies(step):
        p = (r + step) % planes
        here = row16(r)
        return (
            remote(tok_ref.at[:, col(p)], rows_all.at[0, here, pl.ds(0, width)],
                   s_x.at[step], r_x.at[step], x_peer(step)),
            remote(meta_ref, rows_all.at[0, here, pl.ds(width, META)],
                   s_m.at[step], r_m.at[step], x_peer(step)),
        )

    for step in range(1, planes):
        for cp in x_copies(step):
            cp.start()
    own[0].wait()
    own_meta.wait()
    for step in range(1, planes):
        for cp in x_copies(step):
            cp.wait_recv()

    def ag_copy(i):
        return remote(rows_all.at[0], rows_all.at[back[i]], s_ag.at[i], r_ag.at[back[i]], along(order[i], 1 - c, c))

    for i in range(1, ring):
        ag_copy(i).start()

    def w_copies(step):
        p = (r + step) % planes
        here = row16(r, quarter)
        return (
            remote(gate_ref.at[0, :, col(p)], weights.at[0, here, :], s_w.at[0, step], r_w.at[0, step], x_peer(step)),
            remote(up_ref.at[0, :, col(p)], weights.at[1, here, :], s_w.at[1, step], r_w.at[1, step], x_peer(step)),
        )

    for step in range(1, planes):
        for cp in w_copies(step):
            cp.start()

    lanes = msgs * group
    shape = (2 * rows, lanes)
    t = lax.broadcasted_iota(jnp.int32, shape, 0)
    q = lax.broadcasted_iota(jnp.int32, shape, 1)
    j = q // group
    pos, dc = j // 2, j % 2
    d_of = jnp.where(pos % 2 == 1, (pos + 1) // 2, (ring - pos // 2) % ring)
    expert = (2 * ((y + d_of * (1 - c)) % ring) + (c + dc) % 2) * ring + (z + d_of * c) % ring
    expert = expert.astype(F32)
    same_block = (t // rows) == ((q // slots) % 2)
    expert = jnp.where(same_block, expert, -1.0)
    slot_left = ((q % slots) - 2 * ((t // block) % planes)).astype(F32)
    a = lax.broadcasted_iota(jnp.int32, (2 * rows, 2 * rows), 0)
    b = lax.broadcasted_iota(jnp.int32, (2 * rows, 2 * rows), 1)
    earlier = jnp.where((b < a) & (a // block == b // block), 1.0, 0.0).astype(BF)

    def a_copy(k, i, dc):
        return remote(
            outgoing.at[k, 2 * i + dc], arrived.at[k, 2 * back[i] + c],
            s_a.at[k, 2 * i + dc], r_a.at[k, 2 * back[i] + c], along(order[i], c, (c + dc) % 2),
        )

    def own_slots(k):
        return pltpu.make_async_copy(outgoing.at[k, 0], arrived.at[k, c], r_a.at[k, c])

    def place(k):
        for i in (2 * k, 2 * k + 1):
            if i:
                remote(rows_all.at[0], rows_all.at[i], s_ag.at[i], r_ag.at[i], x_peer(1)).wait_recv()
        both = rows_all[2 * k:2 * k + 2].reshape(2 * rows, width + META)
        meta = both[:, width:].astype(F32)
        hits = jnp.zeros(shape, F32)
        high = jnp.zeros(shape, F32)
        low = jnp.zeros(shape, F32)
        for n in range(top):
            named = meta[:, n:n + 1] == expert
            hits = jnp.where(named, 1.0, hits)
            high = jnp.where(named, meta[:, top + n:top + n + 1], high)
            low = jnp.where(named, meta[:, 2 * top + n:2 * top + n + 1], low)
        rank = jnp.dot(earlier, hits.astype(BF), preferred_element_type=F32)
        here = (hits > 0.0) & (rank == slot_left)
        mix_hi[k] = jnp.where(here, high, 0.0).astype(BF)
        mix_lo[k] = jnp.where(here, low, 0.0).astype(BF)
        placed = jnp.where(here, 1.0, 0.0).T.astype(BF)
        sent = jnp.dot(placed, both[:, :width], preferred_element_type=F32).astype(BF)
        outgoing[k] = sent.reshape(msgs, group, width)
        for i in range(ring):
            for dc in range(2):
                if i or dc:
                    a_copy(k, i, dc).start()
        own_slots(k).start()

    def wait_in(buf, sem):
        pltpu.make_async_copy(buf, buf, sem).wait()

    near = (r + 1 - 2 * (r % 2), planes - 1 - r)
    far = (r + 2) % planes

    def plane(p):
        return (p, node, z)

    def p_copy(k, half, n):
        to = near[half]
        return remote(psend.at[k, half, far if n else to], precv.at[k, half, n], s_p.at[k, half, n], r_p.at[k, half, n], plane(to))

    def q_copy(k, half):
        return remote(fwd.at[k, half], frecv.at[k, half], s_q.at[k, half], r_q.at[k, half], plane(near[1 - half]))

    def h_copy(k, n):
        return remote(hid.at[k, r], hid.at[k, r], s_h.at[k, n], r_h.at[k, n], plane(near[n]))

    def g_copy(k, n):
        part = hid.at[k, near[n], :, pl.ds(n * (hidden // 2), hidden // 2)]
        return remote(part, part, s_g.at[k, n], r_g.at[k, n], plane(near[1 - n]))

    def first(k):
        for m in range(msgs):
            wait_in(arrived.at[k, m], r_a.at[k, m])
        x = arrived[k].reshape(msgs * group, width)
        for half in range(2):
            part = lax.dot_general(x, weights[half], (((1,), (1,)), ((), ())), preferred_element_type=F32)
            part = part.reshape(planes, part_rows, hidden)
            pown[k, half] = part
            psend[k, half] = part.astype(BF)
            for n in (1, 0):
                p_copy(k, half, n).start()

    def pass_on(k):
        for half in range(2):
            p_copy(k, half, 1).wait_recv()
            fwd[k, half] = (pown[k, half, near[1 - half]] + precv[k, half, 1].astype(F32)).astype(BF)
            q_copy(k, half).start()

    def second(k):
        sums = []
        for half in range(2):
            p_copy(k, half, 0).wait_recv()
            q_copy(k, half).wait_recv()
            sums.append(pown[k, half, r] + precv[k, half, 0].astype(F32) + frecv[k, half].astype(F32))
        g, u = sums
        hid[k, r] = (g / (1.0 + jnp.exp(-g)) * u).astype(BF)
        for n in range(2):
            h_copy(k, n).start()

    def relay(k):
        for n in range(2):
            wait_in(hid.at[k, near[n]], r_h.at[k, n])
            g_copy(k, n).start()

    def b_copy(k, m):
        i, s = m // 2, m % 2
        dc = (c + s) % 2
        return remote(
            outs.at[k, m], returned.at[k, 2 * back[i] + dc], s_b.at[k, m], r_b.at[k, 2 * back[i] + dc],
            along(order[i], s, s),
        )

    def third(k):
        for n in range(2):
            wait_in(hid.at[k, far, :, pl.ds(n * (hidden // 2), hidden // 2)], r_g.at[k, n])
        h = hid[k].reshape(msgs * group, hidden)
        o = jnp.dot(h, down[...], preferred_element_type=F32).astype(BF)
        outs[k] = o.reshape(msgs, group, width)
        for m in range(msgs):
            if m < 2:
                @pl.when(c != m)
                def _():
                    b_copy(k, m).start()

                @pl.when(c == m)
                def _():
                    pltpu.make_async_copy(outs.at[k, m], returned.at[k, 0], r_b.at[k, 0]).start()
            else:
                b_copy(k, m).start()

    def z_copy(i):
        return remote(zsend.at[i], zrecv.at[back[i]], s_z.at[i], r_z.at[back[i]], along(order[i], 1 - c, c))

    early = [i for i in range(1, ring) if 1 <= back[i] // 2 < chunks - 1]

    def mix(k):
        if k == 0:
            total = jnp.zeros((rows, width), F32)
            for i in early:
                wait_in(zrecv.at[i], r_z.at[i])
                total = total + zrecv[i].astype(F32)
            tsum[...] = total
        for jj in range(msgs):
            wait_in(returned.at[k, jj], r_b.at[k, jj])
        got = returned[k].reshape(lanes, width)
        part = jnp.dot(mix_hi[k], got, preferred_element_type=F32)
        part = part + jnp.dot(mix_lo[k], got, preferred_element_type=F32)
        zsend[2 * k:2 * k + 2] = part.reshape(2, rows, width).astype(BF)
        for i in (2 * k, 2 * k + 1):
            if i:
                z_copy(i).start()

    for k in range(chunks):
        place(k)
    for cp in own[1:]:
        cp.wait()
    for step in range(1, planes):
        for cp in w_copies(step):
            cp.wait_recv()
    stages = []
    for n, k in enumerate([*range(1, chunks), 0]):
        for depth, (late, stage) in enumerate(((0, first), (4, pass_on), (7, second), (10, relay), (13, third), (17, mix))):
            stages.append((3 * n + late, -depth, stage, k))
    for _, _, stage, k in sorted(stages, key=lambda e: e[:2]):
        stage(k)

    total = tsum[...] + zsend[0].astype(F32)
    for i in (i for i in range(1, ring) if i not in early):
        wait_in(zrecv.at[i], r_z.at[i])
        total = total + zrecv[i].astype(F32)
    fin[...] = total.astype(BF).reshape(planes, block, width)

    def f_copy(step):
        p = (r + step) % planes
        return remote(fin.at[p], out_ref.at[:, col(r)], s_f.at[step], r_f.at[step], x_peer(step))

    for step in range(1, planes):
        f_copy(step).start()
    own_cols = pltpu.make_async_copy(fin.at[r], out_ref.at[:, col(r)], l_sem.at[5])
    own_cols.start()

    for step in range(1, planes):
        for cp in x_copies(step) + w_copies(step):
            cp.wait_send()
    for i in range(1, ring):
        ag_copy(i).wait_send()
        z_copy(i).wait_send()
    for k in range(chunks):
        for n in range(2):
            p_copy(k, n, 0).wait_send()
            p_copy(k, n, 1).wait_send()
            q_copy(k, n).wait_send()
            h_copy(k, n).wait_send()
            g_copy(k, n).wait_send()
        for i in range(ring):
            for dc in range(2):
                if i or dc:
                    a_copy(k, i, dc).wait_send()
        for m in range(msgs):
            if m < 2:
                @pl.when(c != m)
                def _():
                    b_copy(k, m).wait_send()
            else:
                b_copy(k, m).wait_send()

    own_cols.wait()
    for step in range(1, planes):
        wait_in(out_ref.at[:, col((r + planes - step) % planes)], r_f.at[step])
    for step in range(1, planes):
        f_copy(step).wait_send()


def on_device(tokens, expert_ids, route_weights, gate_weight, up_weight, down_weight):
    block, top = expert_ids.shape
    planes = lax.axis_size("rep")
    ring = lax.axis_size("local")
    width = down_weight.shape[2]
    hidden = down_weight.shape[1]
    rows, group, msgs = planes * block, planes * 4, 2 * ring
    chunks = ring // 2
    part_rows = msgs * group // planes
    dma = pltpu.SemaphoreType.DMA
    return pl.pallas_call(
        functools.partial(kernel, (planes, ring, block, top, width, hidden)),
        out_shape=jax.ShapeDtypeStruct(tokens.shape, BF),
        in_specs=[pl.BlockSpec(memory_space=pltpu.VMEM)] * 3 + [pl.BlockSpec(memory_space=pl.ANY)] * 3,
        out_specs=pl.BlockSpec(memory_space=pl.ANY),
        scratch_shapes=[
            pltpu.VMEM((block, META), BF),
            pltpu.VMEM((ring, rows, width + META), BF),
            pltpu.VMEM((chunks, msgs, group, width), BF),
            pltpu.VMEM((chunks, msgs, group, width), BF),
            pltpu.VMEM((2, hidden, width), BF),
            pltpu.VMEM((hidden, width), BF),
            pltpu.VMEM((chunks, 2, planes, part_rows, hidden), BF),
            pltpu.VMEM((chunks, 2, planes, part_rows, hidden), F32),
            pltpu.VMEM((chunks, 2, 2, part_rows, hidden), BF),
            pltpu.VMEM((chunks, 2, part_rows, hidden), BF),
            pltpu.VMEM((chunks, 2, part_rows, hidden), BF),
            pltpu.VMEM((chunks, planes, part_rows, hidden), BF),
            pltpu.VMEM((chunks, msgs, group, width), BF),
            pltpu.VMEM((chunks, msgs, group, width), BF),
            pltpu.VMEM((chunks, 2 * rows, msgs * group), BF),
            pltpu.VMEM((chunks, 2 * rows, msgs * group), BF),
            pltpu.VMEM((ring, rows, width), BF),
            pltpu.VMEM((ring, rows, width), BF),
            pltpu.VMEM((planes, block, width), BF),
            pltpu.VMEM((rows, width), F32),
        ]
        + [dma((planes,))] * 4
        + [dma((2, planes))] * 2
        + [dma((ring,))] * 2
        + [dma((chunks, msgs))] * 2
        + [dma((chunks, 2, 2))] * 2
        + [dma((chunks, 2))] * 6
        + [dma((chunks, msgs))] * 2
        + [dma((ring,))] * 2
        + [dma((planes,))] * 2
        + [dma((6,))],
        compiler_params=pltpu.CompilerParams(
            collective_id=0, has_side_effects=True, vmem_limit_bytes=56 * 2**20
        ),
    )(tokens, expert_ids.T, route_weights.T, gate_weight, up_weight, down_weight)


def solution(mesh):
    placed = (
        P(("rep", "node", "local"), None),
        P(("rep", "node", "local"), None),
        P(("rep", "node", "local"), None),
        P(("node", "local"), "rep", None),
        P(("node", "local"), "rep", None),
        P(("node", "local"), None, "rep"),
    )
    return jax.shard_map(
        on_device,
        mesh=mesh,
        in_specs=placed,
        out_specs=P(("rep", "node", "local"), None),
        check_vma=False,
    )
```
